32 devices in a mesh: shot: 32 (over z, y, x, core), freq: 1.
Axes of the slice: x: 2, y: 2, z: 4, core: 2. Of those that a mesh axis runs over, the one named last changes fastest.
Arguments:
- data: bfloat16 [2, 64, 128, 128], P(None, 'freq', 'shot')
- aperture: int32 [128, 64], P('shot'), may hold values from -1 to 127, as said below
- ops: bfloat16 [8, 64, 64], replicated, may hold values from -0.75 to 0.75
- cable_ops: int32 [2], replicated, may hold values from 0 to 7
Outputs:
- multiples: bfloat16 [2, 64, 128, 128], P(None, 'freq', 'shot')
The draws below stay inside these ranges and needn't reach their ends.
Inputs may be any that keep to these rules, and one draw needn't show every extreme that they name: `aperture`: each shot's list holds 1 to 64 distinct surface points first, then -1 padding; some shot's list is full.
All inputs are finite; a program needn't handle non-finite values.
Results may differ from the reference program's by a relative error of at most 0.0004.
Values may be sent and summed in bfloat16 or wider, within the bound.
A program may use at most 64 MiB of HBM per device.

```python
import jax
import jax.numpy as jnp
from jax import lax

APER = 64
CAB = 64
NOPS = 8
N = 128
FREQS = 64
NCAB = 2


def draw_data(key, part):
    first, second = jax.random.split(key, 2)
    shape = (2, FREQS, N, N)
    position = jnp.arange(FREQS, dtype=jnp.float32) / max(FREQS - 1, 1)
    base = jnp.clip(jax.random.normal(first, shape, jnp.float32), -6.0, 6.0)
    ramp = 1.0 + 2.0 * position
    shot_scale = jnp.exp(jax.random.uniform(second, (N,), jnp.float32, 0.0, 2.3))
    values = base * ramp[None, :, None, None] * shot_scale[None, None, :, None]
    return values.astype(jnp.bfloat16)


def draw_aperture(key, part):
    first, second = jax.random.split(key, 2)
    row_keys = jax.random.split(first, N)
    orders = jax.vmap(lambda one_key: jax.random.permutation(one_key, N))(row_keys)[:, :APER].astype(jnp.int32)
    lengths = jax.random.randint(second, (N,), max(APER // 4, 1), APER + 1).astype(jnp.int32)
    lengths = lengths.at[0].set(APER)
    slots = jnp.arange(APER, dtype=jnp.int32)
    return jnp.where(slots[None, :] < lengths[:, None], orders, -1).astype(jnp.int32)


def centred(key, extent, scale, reach, kind=jnp.bfloat16):
    result = jax.random.normal(key, extent, jnp.float32) * scale
    return jnp.minimum(jnp.maximum(result, -reach), reach).astype(kind)


def setup_inputs(seed: int = 0) -> dict:
    key_list = jax.random.split(jax.random.key(seed), 5)
    data = draw_data(jax.random.fold_in(key_list[4], 71), 0)
    aperture = draw_aperture(jax.random.fold_in(key_list[4], 71), 0)
    ops = centred(key_list[2], (NOPS, CAB, CAB), CAB ** -0.5, 0.75)
    cable_ops = jax.random.randint(key_list[3], (NCAB,), 0, NOPS).astype(jnp.int32)
    return {"data": data, "aperture": aperture, "ops": ops, "cable_ops": cable_ops}


def reference(data, aperture, ops, cable_ops):
    highest_value = lax.Precision.HIGHEST
    total = data.shape[3]
    bands = data.shape[1]
    surface = jnp.arange(total, dtype=jnp.int32)
    mask = jnp.any(aperture[:, :, None] == surface[None, None, :], axis=1).astype(jnp.float32)
    values = data.astype(jnp.float32)
    masked_wavefield = values * mask[None, None, :, :]
    chosen = ops[cable_ops].astype(jnp.float32)
    cables = total // CAB
    filtered_traces = jnp.einsum('pfkci,cij->pfkcj', values.reshape(2, bands, total, cables, CAB), chosen, precision=highest_value)
    filtered_traces = filtered_traces.reshape(2, bands, total, total)
    real_part = jnp.einsum('jpy,jyu->jpu', masked_wavefield[0], filtered_traces[0], precision=highest_value) - jnp.einsum('jpy,jyu->jpu', masked_wavefield[1], filtered_traces[1], precision=highest_value)
    imaginary_part = jnp.einsum('jpy,jyu->jpu', masked_wavefield[0], filtered_traces[1], precision=highest_value) + jnp.einsum('jpy,jyu->jpu', masked_wavefield[1], filtered_traces[0], precision=highest_value)
    predicted = jnp.stack([real_part, imaginary_part])
    energy = lax.optimization_barrier(jnp.sum(predicted * predicted, axis=(0, 1, 3)))
    scale = lax.rsqrt(energy / (2.0 * bands * total) + 1e-06)
    return (predicted * scale[None, None, :, None]).astype(jnp.bfloat16)
```

```python
import functools

import jax
import jax.numpy as jnp
from jax import lax
from jax.experimental import pallas as pl
from jax.experimental.pallas import tpu as pltpu
from jax.sharding import PartitionSpec as P

MESH = pl.DeviceIdType.MESH


def kernel(
    n, finish, data, aperture, ops, cable_ops, out,
    dbuf, apbuf, opsbuf, maskbuf, recv, maskrecv, send, back,
    local_sem, send_sem, recv_sem, mask_send_sem, mask_recv_sem, back_send_sem, back_recv_sem,
):
    me = lax.axis_index("shot")
    parts, freqs, shots, traces = data.shape
    mine = freqs // n
    total = n * shots
    cables = cable_ops.shape[0]
    width = ops.shape[1]

    barrier = pltpu.get_barrier_semaphore()

    def greet(i, carry):
        pl.semaphore_signal(barrier, inc=1, device_id={"shot": lax.rem(me + i, n)}, device_id_type=MESH)
        return carry

    lax.fori_loop(1, n, greet, 0)

    fetches = [
        pltpu.make_async_copy(aperture, apbuf, local_sem.at[0]),
        pltpu.make_async_copy(data, dbuf, local_sem.at[1]),
        pltpu.make_async_copy(ops, opsbuf, local_sem.at[2]),
    ]
    for fetch in fetches:
        fetch.start()

    fetches[0].wait()
    lists = apbuf[...]
    surface = lax.broadcasted_iota(jnp.int32, (shots, total), 1)
    found = jnp.zeros((shots, total), jnp.float32)
    for a in range(lists.shape[1]):
        found = jnp.where(lists[:, a : a + 1] == surface, 1.0, found)
    maskbuf[...] = found.astype(jnp.bfloat16)
    fetches[1].wait()
    fetches[2].wait()

    pl.semaphore_wait(barrier, n - 1)

    def scatter(i, carry):
        peer = lax.rem(me + i, n)
        pltpu.make_async_remote_copy(
            src_ref=maskbuf, dst_ref=maskrecv.at[me], send_sem=mask_send_sem, recv_sem=mask_recv_sem,
            device_id={"shot": peer}, device_id_type=MESH,
        ).start()
        pltpu.make_async_remote_copy(
            src_ref=dbuf.at[:, pl.ds(peer * mine, mine)], dst_ref=recv.at[me],
            send_sem=send_sem, recv_sem=recv_sem,
            device_id={"shot": peer}, device_id_type=MESH,
        ).start()
        return carry

    lax.fori_loop(1, n, scatter, 0)
    pltpu.make_async_copy(maskbuf, maskrecv.at[me], mask_recv_sem).start()
    pltpu.make_async_copy(dbuf.at[:, pl.ds(me * mine, mine)], recv.at[me], recv_sem).start()

    rows = []
    for c in range(cables):
        pieces = [jnp.zeros((width, width), jnp.float32)] * cables
        pieces[c] = opsbuf[cable_ops[c]].astype(jnp.float32)
        rows.append(jnp.concatenate(pieces, axis=1))
    operator = jnp.concatenate(rows, axis=0).astype(jnp.bfloat16)

    pltpu.make_async_copy(maskrecv, maskrecv, mask_recv_sem).wait()
    mask = maskrecv[...].astype(jnp.float32).reshape(total, total)
    pltpu.make_async_copy(recv, recv, recv_sem).wait()

    for f in range(mine):
        real = recv[:, 0, f].astype(jnp.float32).reshape(total, traces)
        imag = recv[:, 1, f].astype(jnp.float32).reshape(total, traces)
        left = jnp.concatenate([real * mask, imag * mask], axis=1).astype(jnp.bfloat16)
        right = jnp.concatenate(
            [jnp.concatenate([real, imag], axis=1), jnp.concatenate([-imag, real], axis=1)], axis=0
        ).astype(jnp.bfloat16)
        product = jnp.dot(left, right, preferred_element_type=jnp.float32)
        product = jnp.concatenate([product[:, :traces], product[:, traces:]], axis=0)
        high = product.astype(jnp.bfloat16)
        rest = product - high.astype(jnp.float32)
        middle = rest.astype(jnp.bfloat16)
        low = (rest - middle.astype(jnp.float32)).astype(jnp.bfloat16)
        result = jnp.dot(low, operator, preferred_element_type=jnp.float32)
        result += jnp.dot(middle, operator, preferred_element_type=jnp.float32)
        result += jnp.dot(high, operator, preferred_element_type=jnp.float32)
        result = result.reshape(parts, n, shots, traces)
        for p in range(parts):
            send[:, p, f] = result[p]

    def gather(i, carry):
        peer = lax.rem(me + i, n)
        pltpu.make_async_remote_copy(
            src_ref=send.at[peer], dst_ref=back.at[:, pl.ds(me * mine, mine)],
            send_sem=back_send_sem, recv_sem=back_recv_sem,
            device_id={"shot": peer}, device_id_type=MESH,
        ).start()
        return carry

    lax.fori_loop(1, n, gather, 0)
    pltpu.make_async_copy(send.at[me], back.at[:, pl.ds(me * mine, mine)], back_recv_sem).start()

    others = pl.ds(0, n - 1)
    pltpu.make_async_copy(maskrecv.at[others], maskrecv.at[others], mask_send_sem).wait()
    pltpu.make_async_copy(recv.at[others], recv.at[others], send_sem).wait()
    pltpu.make_async_copy(back, back, back_recv_sem).wait()
    if finish:
        predicted = back[...]
        energy = jnp.sum(jnp.sum(predicted * predicted, axis=(0, 1)), axis=1, keepdims=True)
        scale = lax.rsqrt(energy / (2.0 * freqs * traces) + 1e-06)
        out[...] = (predicted * scale[None, None]).astype(out.dtype)
    pltpu.make_async_copy(send.at[others], send.at[others], back_send_sem).wait()


def per_device(n, bands, data, aperture, ops, cable_ops):
    parts, freqs, shots, traces = data.shape
    mine = freqs // n
    finish = bands == 1
    dma = pltpu.SemaphoreType.DMA
    shape = (parts, freqs, shots, traces)
    scratch = [
        pltpu.VMEM(data.shape, data.dtype),
        pltpu.VMEM(aperture.shape, aperture.dtype),
        pltpu.VMEM(ops.shape, ops.dtype),
        pltpu.VMEM((shots, n * shots), jnp.bfloat16),
        pltpu.VMEM((n, parts, mine, shots, traces), jnp.bfloat16),
        pltpu.VMEM((n, shots, n * shots), jnp.bfloat16),
        pltpu.VMEM((n, parts, mine, shots, traces), jnp.float32),
    ]
    sems = [dma((3,))] + [dma] * 6
    anywhere = pl.BlockSpec(memory_space=pl.ANY)
    body = functools.partial(kernel, n, finish)
    if finish:
        scratch.append(pltpu.VMEM(shape, jnp.float32))
        out_dtype = jnp.bfloat16
    else:
        inner = body

        def body(data, aperture, ops, cable_ops, out, *rest):
            held = len(scratch)
            inner(data, aperture, ops, cable_ops, out, *rest[:held], out, *rest[held:])

        out_dtype = jnp.float32
    result = pl.pallas_call(
        body,
        out_shape=jax.ShapeDtypeStruct(shape, out_dtype),
        in_specs=[anywhere, anywhere, anywhere, pl.BlockSpec(memory_space=pltpu.SMEM)],
        out_specs=pl.BlockSpec(memory_space=pltpu.VMEM),
        scratch_shapes=scratch + sems,
        compiler_params=pltpu.CompilerParams(collective_id=0, has_side_effects=True),
        name="predict",
    )(data, aperture, ops, cable_ops)
    if finish:
        return result
    energy = lax.psum(jnp.sum(result * result, axis=(0, 1, 3)), "freq")
    scale = lax.rsqrt(energy / (2.0 * freqs * bands * traces) + 1e-06)
    return (result * scale[None, None, :, None]).astype(jnp.bfloat16)


def solution(mesh):
    return jax.shard_map(
        functools.partial(per_device, mesh.shape["shot"], mesh.shape["freq"]),
        mesh=mesh,
        in_specs=(P(None, "freq", "shot", None), P("shot", None), P(), P()),
        out_specs=P(None, "freq", "shot", None),
        check_vma=False,
    )
```

```python
import functools

import jax
import jax.numpy as jnp
from jax import lax
from jax.experimental import pallas as pl
from jax.experimental.pallas import tpu as pltpu
from jax.sharding import PartitionSpec as P

MESH = pl.DeviceIdType.MESH


def kernel(
    n, groups, chunks, finish, data, aperture, ops, cable_ops, out,
    dbuf, apbuf, opsbuf, maskbuf, recv, maskrecv, send, back,
    local_sem, recv_sem, send_sem, mask_send_sem, mask_recv_sem, back_send_sem, back_recv_sem,
):
    me = lax.axis_index("shot")
    parts, freqs, shots, traces = data.shape
    team = n // groups
    per = freqs // (team * chunks)
    total, rows = n * shots, team * shots
    cables = cable_ops.shape[0]
    width = ops.shape[1]
    seat = lax.rem(me, team)
    first = me - seat

    barrier = pltpu.get_barrier_semaphore()

    def greet(i, carry):
        pl.semaphore_signal(barrier, inc=1, device_id={"shot": lax.rem(me + i, n)}, device_id_type=MESH)
        return carry

    lax.fori_loop(1, n, greet, 0)

    fetches = [
        pltpu.make_async_copy(aperture, apbuf, local_sem.at[0]),
        pltpu.make_async_copy(data, dbuf, local_sem.at[1]),
        pltpu.make_async_copy(ops, opsbuf, local_sem.at[2]),
    ]
    for fetch in fetches:
        fetch.start()

    fetches[0].wait()
    lists = apbuf[...]
    surface = lax.broadcasted_iota(jnp.int32, (shots, total), 1)
    found = jnp.zeros((shots, total), jnp.float32)
    for a in range(lists.shape[1]):
        found = jnp.where(lists[:, a : a + 1] == surface, 1.0, found)
    maskbuf[...] = found.astype(jnp.bfloat16)
    fetches[1].wait()
    fetches[2].wait()

    pl.semaphore_wait(barrier, n - 1)

    def block(chunk, peer_seat):
        return dbuf.at[:, pl.ds((peer_seat * chunks + chunk) * per, per)]

    def team_peer(i):
        peer_seat = lax.rem(seat + i, team)
        return peer_seat, first + peer_seat

    def scatter(chunk, peer_seat, peer):
        pltpu.make_async_remote_copy(
            src_ref=block(chunk, peer_seat), dst_ref=recv.at[chunk, me],
            send_sem=send_sem, recv_sem=recv_sem.at[chunk],
            device_id={"shot": peer}, device_id_type=MESH,
        ).start()

    for chunk in range(chunks):

        def abroad(i, carry):
            peer_seat = lax.rem(seat + lax.rem(i, team), team)
            peer = lax.rem(first + team * (1 + i // team), n) + peer_seat
            scatter(chunk, peer_seat, peer)
            return carry

        def home(i, carry):
            peer_seat, peer = team_peer(i)
            if chunk == 0:
                pltpu.make_async_remote_copy(
                    src_ref=maskbuf, dst_ref=maskrecv.at[seat],
                    send_sem=mask_send_sem, recv_sem=mask_recv_sem,
                    device_id={"shot": peer}, device_id_type=MESH,
                ).start()
            scatter(chunk, peer_seat, peer)
            return carry

        lax.fori_loop(0, n - team, abroad, 0)
        lax.fori_loop(1, team, home, 0)
        if chunk == 0:
            pltpu.make_async_copy(maskbuf, maskrecv.at[seat], mask_recv_sem).start()
        pltpu.make_async_copy(block(chunk, seat), recv.at[chunk, me], recv_sem.at[chunk]).start()

    lines = []
    for c in range(cables):
        pieces = [jnp.zeros((width, width), jnp.float32)] * cables
        pieces[c] = opsbuf[cable_ops[c]].astype(jnp.float32)
        lines.append(jnp.concatenate(pieces, axis=1))
    operator = jnp.concatenate(lines, axis=0).astype(jnp.bfloat16)

    pltpu.make_async_copy(maskrecv, maskrecv, mask_recv_sem).wait()
    mask = maskrecv[...].astype(jnp.float32).reshape(rows, total)

    for chunk in range(chunks):
        pltpu.make_async_copy(recv.at[chunk], recv.at[chunk], recv_sem.at[chunk]).wait()
        for f in range(per):
            real = recv[chunk, :, 0, f].astype(jnp.float32).reshape(total, traces)
            imag = recv[chunk, :, 1, f].astype(jnp.float32).reshape(total, traces)
            if groups == 1:
                own_real, own_imag = real, imag
            else:
                own_real = recv[chunk, pl.ds(first, team), 0, f].astype(jnp.float32).reshape(rows, traces)
                own_imag = recv[chunk, pl.ds(first, team), 1, f].astype(jnp.float32).reshape(rows, traces)
            left = jnp.concatenate([own_real * mask, own_imag * mask], axis=1).astype(jnp.bfloat16)
            right = jnp.concatenate(
                [jnp.concatenate([real, imag], axis=1), jnp.concatenate([-imag, real], axis=1)], axis=0
            ).astype(jnp.bfloat16)
            product = jnp.dot(left, right, preferred_element_type=jnp.float32)
            product = jnp.concatenate([product[:, :traces], product[:, traces:]], axis=0)
            high = product.astype(jnp.bfloat16)
            rest = product - high.astype(jnp.float32)
            middle = rest.astype(jnp.bfloat16)
            low = (rest - middle.astype(jnp.float32)).astype(jnp.bfloat16)
            result = jnp.dot(low, operator, preferred_element_type=jnp.float32)
            result += jnp.dot(middle, operator, preferred_element_type=jnp.float32)
            result += jnp.dot(high, operator, preferred_element_type=jnp.float32)
            result = result.reshape(parts, team, shots, traces)
            for p in range(parts):
                send[chunk, :, p, f] = result[p]

        landing = back.at[:, pl.ds((seat * chunks + chunk) * per, per)]

        def gather(i, carry):
            peer_seat, peer = team_peer(i)
            pltpu.make_async_remote_copy(
                src_ref=send.at[chunk, peer_seat], dst_ref=landing,
                send_sem=back_send_sem, recv_sem=back_recv_sem,
                device_id={"shot": peer}, device_id_type=MESH,
            ).start()
            return carry

        lax.fori_loop(1, team, gather, 0)
        pltpu.make_async_copy(send.at[chunk, seat], landing, back_recv_sem).start()

    mask_sent = maskrecv.at[pl.ds(0, team - 1)]
    sent = recv.at[:, pl.ds(0, n - 1)]
    back_sent = send.at[:, pl.ds(0, team - 1)]
    pltpu.make_async_copy(mask_sent, mask_sent, mask_send_sem).wait()
    pltpu.make_async_copy(sent, sent, send_sem).wait()
    pltpu.make_async_copy(back, back, back_recv_sem).wait()
    if finish:
        predicted = back[...]
        energy = jnp.sum(jnp.sum(predicted * predicted, axis=(0, 1)), axis=1, keepdims=True)
        scale = lax.rsqrt(energy / (2.0 * freqs * traces) + 1e-06)
        out[...] = (predicted * scale[None, None]).astype(out.dtype)
    pltpu.make_async_copy(back_sent, back_sent, back_send_sem).wait()


GROUPS = 2
CHUNKS = 2


def per_device(n, bands, data, aperture, ops, cable_ops):
    parts, freqs, shots, traces = data.shape
    groups, chunks = GROUPS, CHUNKS
    team = n // groups
    per = freqs // (team * chunks)
    finish = bands == 1
    dma = pltpu.SemaphoreType.DMA
    shape = (parts, freqs, shots, traces)
    scratch = [
        pltpu.VMEM(data.shape, data.dtype),
        pltpu.VMEM(aperture.shape, aperture.dtype),
        pltpu.VMEM(ops.shape, ops.dtype),
        pltpu.VMEM((shots, n * shots), jnp.bfloat16),
        pltpu.VMEM((chunks, n, parts, per, shots, traces), jnp.bfloat16),
        pltpu.VMEM((team, shots, n * shots), jnp.bfloat16),
        pltpu.VMEM((chunks, team, parts, per, shots, traces), jnp.float32),
    ]
    sems = [dma((3,)), dma((chunks,))] + [dma] * 5
    anywhere = pl.BlockSpec(memory_space=pl.ANY)
    body = functools.partial(kernel, n, groups, chunks, finish)
    if finish:
        scratch.append(pltpu.VMEM(shape, jnp.float32))
        out_dtype = jnp.bfloat16
    else:
        inner = body

        def body(data, aperture, ops, cable_ops, out, *rest):
            held = len(scratch)
            inner(data, aperture, ops, cable_ops, out, *rest[:held], out, *rest[held:])

        out_dtype = jnp.float32
    result = pl.pallas_call(
        body,
        out_shape=jax.ShapeDtypeStruct(shape, out_dtype),
        in_specs=[anywhere, anywhere, anywhere, pl.BlockSpec(memory_space=pltpu.SMEM)],
        out_specs=pl.BlockSpec(memory_space=pltpu.VMEM),
        scratch_shapes=scratch + sems,
        compiler_params=pltpu.CompilerParams(collective_id=0, has_side_effects=True),
        name="predict",
    )(data, aperture, ops, cable_ops)
    if finish:
        return result
    energy = lax.psum(jnp.sum(result * result, axis=(0, 1, 3)), "freq")
    scale = lax.rsqrt(energy / (2.0 * freqs * bands * traces) + 1e-06)
    return (result * scale[None, None, :, None]).astype(jnp.bfloat16)


def solution(mesh):
    return jax.shard_map(
        functools.partial(per_device, mesh.shape["shot"], mesh.shape["freq"]),
        mesh=mesh,
        in_specs=(P(None, "freq", "shot", None), P("shot", None), P(), P()),
        out_specs=P(None, "freq", "shot", None),
        check_vma=False,
    )
```

```python
import functools

import jax
import jax.numpy as jnp
from jax import lax
from jax.experimental import pallas as pl
from jax.experimental.pallas import tpu as pltpu
from jax.sharding import PartitionSpec as P

MESH = pl.DeviceIdType.MESH


def kernel(
    n, groups, chunks, finish, data, aperture, ops, cable_ops, out,
    dbuf, apbuf, opsbuf, maskbuf, recv, maskrecv, send, back,
    local_sem, recv_sem, send_sem, mask_send_sem, mask_recv_sem, back_send_sem, back_recv_sem, team_sem,
):
    me = lax.axis_index("shot")
    parts, blocks, per, shots, traces = data.shape
    team = n // groups
    freqs = blocks * per
    total, rows = n * shots, team * shots
    cables = cable_ops.shape[0]
    width = ops.shape[1]
    seat = lax.rem(me, team)
    first = me - seat

    flips = []
    for place in (1 << k for k in range(n.bit_length() - 1)):
        flips.append((place, place * (1 - 2 * lax.rem(me // place, 2))))

    def partner(m):
        return me + sum(flip for place, flip in flips if m & place)

    def partner_seat(m):
        return seat + sum(flip for place, flip in flips if m & place and place < team)

    barrier = pltpu.get_barrier_semaphore()
    for m in reversed(range(team, n)):
        pl.semaphore_signal(barrier, inc=1, device_id={"shot": partner(m)}, device_id_type=MESH)

    fetches = [
        pltpu.make_async_copy(aperture, apbuf, local_sem.at[0]),
        pltpu.make_async_copy(ops, opsbuf, local_sem.at[1]),
    ] + [pltpu.make_async_copy(data.at[p], dbuf.at[:, p], local_sem.at[2 + p]) for p in range(parts)]
    for fetch in fetches:
        fetch.start()

    fetches[0].wait()
    lists = apbuf[...]
    surface = lax.broadcasted_iota(jnp.int32, (shots, total), 1)
    found = jnp.zeros((shots, total), jnp.float32)
    for a in range(lists.shape[1]):
        found = jnp.where(lists[:, a : a + 1] == surface, 1.0, found)
    maskbuf[...] = found.astype(jnp.bfloat16)
    for fetch in fetches[1:]:
        fetch.wait()

    pl.semaphore_wait(barrier, n - team)
    pl.semaphore_signal(team_sem, inc=1, device_id={"shot": partner(team)}, device_id_type=MESH)

    def block(chunk, peer_seat):
        return dbuf.at[peer_seat * chunks + chunk]

    def scatter(chunk, peer_seat, peer):
        pltpu.make_async_remote_copy(
            src_ref=block(chunk, peer_seat), dst_ref=recv.at[chunk, me],
            send_sem=send_sem, recv_sem=recv_sem.at[chunk],
            device_id={"shot": peer}, device_id_type=MESH,
        ).start()

    for chunk in range(chunks):
        for m in reversed(range(1, n)):
            if chunk == 0 and m == team - 1:
                pl.semaphore_wait(team_sem, 1)
            if chunk == 0 and m < team:
                pltpu.make_async_remote_copy(
                    src_ref=maskbuf, dst_ref=maskrecv.at[seat],
                    send_sem=mask_send_sem, recv_sem=mask_recv_sem,
                    device_id={"shot": partner(m)}, device_id_type=MESH,
                ).start()
            scatter(chunk, partner_seat(m), partner(m))
        if chunk == 0:
            pltpu.make_async_copy(maskbuf, maskrecv.at[seat], mask_recv_sem).start()
        pltpu.make_async_copy(block(chunk, seat), recv.at[chunk, me], recv_sem.at[chunk]).start()

    lines = []
    for c in range(cables):
        pieces = [jnp.zeros((width, width), jnp.float32)] * cables
        pieces[c] = opsbuf[cable_ops[c]].astype(jnp.float32)
        lines.append(jnp.concatenate(pieces, axis=1))
    operator = jnp.concatenate(lines, axis=0).astype(jnp.bfloat16)

    pltpu.make_async_copy(maskrecv, maskrecv, mask_recv_sem).wait()
    mask = maskrecv[...].astype(jnp.float32).reshape(rows, total)

    for chunk in range(chunks):
        pltpu.make_async_copy(recv.at[chunk], recv.at[chunk], recv_sem.at[chunk]).wait()
        for f in range(per):
            real = recv[chunk, :, 0, f].astype(jnp.float32).reshape(total, traces)
            imag = recv[chunk, :, 1, f].astype(jnp.float32).reshape(total, traces)
            if groups == 1:
                own_real, own_imag = real, imag
            else:
                own_real = recv[chunk, pl.ds(first, team), 0, f].astype(jnp.float32).reshape(rows, traces)
                own_imag = recv[chunk, pl.ds(first, team), 1, f].astype(jnp.float32).reshape(rows, traces)
            left = jnp.concatenate([own_real * mask, own_imag * mask], axis=1).astype(jnp.bfloat16)
            right = jnp.concatenate(
                [jnp.concatenate([real, imag], axis=1), jnp.concatenate([-imag, real], axis=1)], axis=0
            ).astype(jnp.bfloat16)
            product = jnp.dot(left, right, preferred_element_type=jnp.float32)
            product = jnp.concatenate([product[:, :traces], product[:, traces:]], axis=0)
            high = product.astype(jnp.bfloat16)
            rest = product - high.astype(jnp.float32)
            middle = rest.astype(jnp.bfloat16)
            low = (rest - middle.astype(jnp.float32)).astype(jnp.bfloat16)
            result = jnp.dot(low, operator, preferred_element_type=jnp.float32)
            result += jnp.dot(middle, operator, preferred_element_type=jnp.float32)
            result += jnp.dot(high, operator, preferred_element_type=jnp.float32)
            result = result.reshape(parts, team, shots, traces)
            for p in range(parts):
                send[chunk, :, p, f] = result[p]

        landing = back.at[seat * chunks + chunk]

        for m in reversed(range(1, team)):
            pltpu.make_async_remote_copy(
                src_ref=send.at[chunk, partner_seat(m)], dst_ref=landing,
                send_sem=back_send_sem, recv_sem=back_recv_sem,
                device_id={"shot": partner(m)}, device_id_type=MESH,
            ).start()
        pltpu.make_async_copy(send.at[chunk, seat], landing, back_recv_sem).start()

    mask_sent = maskrecv.at[pl.ds(0, team - 1)]
    sent = recv.at[:, pl.ds(0, n - 1)]
    back_sent = send.at[:, pl.ds(0, team - 1)]
    pltpu.make_async_copy(mask_sent, mask_sent, mask_send_sem).wait()
    pltpu.make_async_copy(sent, sent, send_sem).wait()
    pltpu.make_async_copy(back, back, back_recv_sem).wait()
    if finish:
        predicted = back[...]
        energy = jnp.sum(jnp.sum(predicted * predicted, axis=(0, 1, 2)), axis=1, keepdims=True)
        scale = lax.rsqrt(energy / (2.0 * freqs * traces) + 1e-06)
        for p in range(parts):
            out[p] = (back[:, p] * scale[None, None]).astype(out.dtype)
    pltpu.make_async_copy(back_sent, back_sent, back_send_sem).wait()


GROUPS = 2
CHUNKS = 2


def per_device(n, bands, data, aperture, ops, cable_ops):
    parts, freqs, shots, traces = data.shape
    groups, chunks = GROUPS, CHUNKS
    team = n // groups
    per = freqs // (team * chunks)
    finish = bands == 1
    dma = pltpu.SemaphoreType.DMA
    blocks = team * chunks
    held = (blocks, parts, per, shots, traces)
    shape = (parts, blocks, per, shots, traces) if finish else held
    scratch = [
        pltpu.VMEM(held, data.dtype),
        pltpu.VMEM(aperture.shape, aperture.dtype),
        pltpu.VMEM(ops.shape, ops.dtype),
        pltpu.VMEM((shots, n * shots), jnp.bfloat16),
        pltpu.VMEM((chunks, n, parts, per, shots, traces), jnp.bfloat16),
        pltpu.VMEM((team, shots, n * shots), jnp.bfloat16),
        pltpu.VMEM((chunks, team, parts, per, shots, traces), jnp.float32),
    ]
    sems = [dma((2 + parts,)), dma((chunks,))] + [dma] * 5 + [pltpu.SemaphoreType.REGULAR]
    anywhere = pl.BlockSpec(memory_space=pl.ANY)
    body = functools.partial(kernel, n, groups, chunks, finish)
    if finish:
        scratch.append(pltpu.VMEM(held, jnp.float32))
        out_dtype = jnp.bfloat16
    else:
        inner = body

        def body(data, aperture, ops, cable_ops, out, *rest):
            place = len(scratch)
            inner(data, aperture, ops, cable_ops, out, *rest[:place], out, *rest[place:])

        out_dtype = jnp.float32
    result = pl.pallas_call(
        body,
        out_shape=jax.ShapeDtypeStruct(shape, out_dtype),
        in_specs=[anywhere, anywhere, anywhere, pl.BlockSpec(memory_space=pltpu.SMEM)],
        out_specs=pl.BlockSpec(memory_space=pltpu.VMEM),
        scratch_shapes=scratch + sems,
        compiler_params=pltpu.CompilerParams(collective_id=0, has_side_effects=True),
        name="predict",
    )(data.reshape(parts, blocks, per, shots, traces), aperture, ops, cable_ops)
    if finish:
        return result.reshape(data.shape)
    result = jnp.swapaxes(result, 0, 1).reshape(data.shape)
    energy = lax.psum(jnp.sum(result * result, axis=(0, 1, 3)), "freq")
    scale = lax.rsqrt(energy / (2.0 * freqs * bands * traces) + 1e-06)
    return (result * scale[None, None, :, None]).astype(jnp.bfloat16)


def solution(mesh):
    return jax.shard_map(
        functools.partial(per_device, mesh.shape["shot"], mesh.shape["freq"]),
        mesh=mesh,
        in_specs=(P(None, "freq", "shot", None), P("shot", None), P(), P()),
        out_specs=P(None, "freq", "shot", None),
        check_vma=False,
    )
```

```python
import functools

import jax
import jax.numpy as jnp
from jax import lax
from jax.experimental import pallas as pl
from jax.experimental.pallas import tpu as pltpu
from jax.sharding import PartitionSpec as P

MESH = pl.DeviceIdType.MESH


def kernel(
    n, groups, chunks, finish, data, aperture, ops, cable_ops, out,
    dbuf, apbuf, opsbuf, maskbuf, recv, maskrecv, send, back,
    local_sem, recv_sem, send_sem, mask_send_sem, mask_recv_sem, back_send_sem, back_recv_sem, team_sem,
):
    me = lax.axis_index("shot")
    parts, blocks, per, shots, traces = data.shape
    team = n // groups
    freqs = blocks * per
    total, rows = n * shots, team * shots
    cables = cable_ops.shape[0]
    width = ops.shape[1]
    seat = lax.rem(me, team)
    first = me - seat

    flips = []
    for place in (1 << k for k in range(n.bit_length() - 1)):
        flips.append((place, place * (1 - 2 * lax.rem(me // place, 2))))

    def partner(m):
        return me + sum(flip for place, flip in flips if m & place)

    def partner_seat(m):
        return seat + sum(flip for place, flip in flips if m & place and place < team)

    barrier = pltpu.get_barrier_semaphore()
    for m in reversed(range(team, n)):
        pl.semaphore_signal(barrier, inc=1, device_id={"shot": partner(m)}, device_id_type=MESH)

    fetches = [
        pltpu.make_async_copy(aperture, apbuf, local_sem.at[0]),
        pltpu.make_async_copy(ops, opsbuf, local_sem.at[1]),
    ] + [pltpu.make_async_copy(data.at[p], dbuf.at[:, p], local_sem.at[2 + p]) for p in range(parts)]
    for fetch in fetches:
        fetch.start()

    fetches[0].wait()
    lists = apbuf[...]
    surface = lax.broadcasted_iota(jnp.int32, (shots, total), 1)
    found = jnp.zeros((shots, total), jnp.float32)
    for a in range(lists.shape[1]):
        found = jnp.where(lists[:, a : a + 1] == surface, 1.0, found)
    maskbuf[...] = found.astype(jnp.bfloat16)
    for fetch in fetches[1:]:
        fetch.wait()

    pl.semaphore_wait(barrier, n - team)
    pl.semaphore_signal(team_sem, inc=1, device_id={"shot": partner(team)}, device_id_type=MESH)

    def block(chunk, peer_seat):
        return dbuf.at[peer_seat * chunks + chunk]

    def scatter(chunk, peer_seat, peer):
        pltpu.make_async_remote_copy(
            src_ref=block(chunk, peer_seat), dst_ref=recv.at[chunk, me],
            send_sem=send_sem, recv_sem=recv_sem.at[chunk],
            device_id={"shot": peer}, device_id_type=MESH,
        ).start()

    for chunk in range(chunks):
        for m in reversed(range(1, n)):
            if chunk == 0 and m == team - 1:
                pl.semaphore_wait(team_sem, 1)
            if chunk == 0 and m < team:
                pltpu.make_async_remote_copy(
                    src_ref=maskbuf, dst_ref=maskrecv.at[seat],
                    send_sem=mask_send_sem, recv_sem=mask_recv_sem,
                    device_id={"shot": partner(m)}, device_id_type=MESH,
                ).start()
            scatter(chunk, partner_seat(m), partner(m))
        if chunk == 0:
            pltpu.make_async_copy(maskbuf, maskrecv.at[seat], mask_recv_sem).start()
        pltpu.make_async_copy(block(chunk, seat), recv.at[chunk, me], recv_sem.at[chunk]).start()

    lines = []
    for c in range(cables):
        pieces = [jnp.zeros((width, width), jnp.float32)] * cables
        pieces[c] = opsbuf[cable_ops[c]].astype(jnp.float32)
        lines.append(jnp.concatenate(pieces, axis=1))
    operator = jnp.concatenate(lines, axis=0).astype(jnp.bfloat16)

    pltpu.make_async_copy(maskrecv, maskrecv, mask_recv_sem).wait()
    mask = maskrecv[...].astype(jnp.float32).reshape(rows, total)

    for chunk in range(chunks):
        pltpu.make_async_copy(recv.at[chunk], recv.at[chunk], recv_sem.at[chunk]).wait()
        for f in range(per):
            real = recv[chunk, :, 0, f].astype(jnp.float32).reshape(total, traces)
            imag = recv[chunk, :, 1, f].astype(jnp.float32).reshape(total, traces)
            if groups == 1:
                own_real, own_imag = real, imag
            else:
                own_real = recv[chunk, pl.ds(first, team), 0, f].astype(jnp.float32).reshape(rows, traces)
                own_imag = recv[chunk, pl.ds(first, team), 1, f].astype(jnp.float32).reshape(rows, traces)
            left = jnp.concatenate([own_real * mask, own_imag * mask], axis=1).astype(jnp.bfloat16)
            right = jnp.concatenate(
                [jnp.concatenate([real, imag], axis=1), jnp.concatenate([-imag, real], axis=1)], axis=0
            ).astype(jnp.bfloat16)
            product = jnp.dot(left, right, preferred_element_type=jnp.float32)
            product = jnp.concatenate([product[:, :traces], product[:, traces:]], axis=0)
            high = product.astype(jnp.bfloat16)
            rest = product - high.astype(jnp.float32)
            middle = rest.astype(jnp.bfloat16)
            low = (rest - middle.astype(jnp.float32)).astype(jnp.bfloat16)
            result = jnp.dot(low, operator, preferred_element_type=jnp.float32)
            result += jnp.dot(middle, operator, preferred_element_type=jnp.float32)
            result += jnp.dot(high, operator, preferred_element_type=jnp.float32)
            result = result.reshape(parts, team, shots, traces)
            for p in range(parts):
                send[chunk, :, p, f] = result[p]

        landing = back.at[seat * chunks + chunk]

        for m in reversed(range(1, team)):
            pltpu.make_async_remote_copy(
                src_ref=send.at[chunk, partner_seat(m)], dst_ref=landing,
                send_sem=back_send_sem, recv_sem=back_recv_sem,
                device_id={"shot": partner(m)}, device_id_type=MESH,
            ).start()
        pltpu.make_async_copy(send.at[chunk, seat], landing, back_recv_sem).start()

    mask_sent = maskrecv.at[pl.ds(0, team - 1)]
    sent = recv.at[:, pl.ds(0, n - 1)]
    back_sent = send.at[:, pl.ds(0, team - 1)]
    pltpu.make_async_copy(mask_sent, mask_sent, mask_send_sem).wait()
    pltpu.make_async_copy(sent, sent, send_sem).wait()
    pltpu.make_async_copy(back, back, back_recv_sem).wait()
    if finish:
        predicted = back[...]
        energy = jnp.sum(jnp.sum(predicted * predicted, axis=(0, 1, 2)), axis=1, keepdims=True)
        scale = lax.rsqrt(energy / (2.0 * freqs * traces) + 1e-06)
        for p in range(parts):
            out[p] = (back[:, p] * scale[None, None]).astype(out.dtype)
    pltpu.make_async_copy(back_sent, back_sent, back_send_sem).wait()


GROUPS = 2
CHUNKS = 2


def per_device(n, bands, data, aperture, ops, cable_ops):
    parts, freqs, shots, traces = data.shape
    groups, chunks = GROUPS, CHUNKS
    team = n // groups
    per = freqs // (team * chunks)
    finish = bands == 1
    dma = pltpu.SemaphoreType.DMA
    blocks = team * chunks
    held = (blocks, parts, per, shots, traces)
    shape = (parts, blocks, per, shots, traces) if finish else held
    scratch = [
        pltpu.VMEM(held, data.dtype),
        pltpu.VMEM(aperture.shape, aperture.dtype),
        pltpu.VMEM(ops.shape, ops.dtype),
        pltpu.VMEM((shots, n * shots), jnp.bfloat16),
        pltpu.VMEM((chunks, n, parts, per, shots, traces), jnp.bfloat16),
        pltpu.VMEM((team, shots, n * shots), jnp.bfloat16),
        pltpu.VMEM((chunks, team, parts, per, shots, traces), jnp.float32),
    ]
    sems = [dma((2 + parts,)), dma((chunks,))] + [dma] * 5 + [pltpu.SemaphoreType.REGULAR]
    anywhere = pl.BlockSpec(memory_space=pl.ANY)
    body = functools.partial(kernel, n, groups, chunks, finish)
    if finish:
        scratch.append(pltpu.VMEM(held, jnp.float32))
        out_dtype = jnp.bfloat16
    else:
        inner = body

        def body(data, aperture, ops, cable_ops, out, *rest):
            place = len(scratch)
            inner(data, aperture, ops, cable_ops, out, *rest[:place], out, *rest[place:])

        out_dtype = jnp.float32
    result = pl.pallas_call(
        body,
        out_shape=pltpu.VMEM(shape, out_dtype),
        in_specs=[anywhere, anywhere, anywhere, pl.BlockSpec(memory_space=pltpu.SMEM)],
        out_specs=pl.BlockSpec(memory_space=pltpu.VMEM),
        scratch_shapes=scratch + sems,
        compiler_params=pltpu.CompilerParams(collective_id=0, has_side_effects=True),
        name="predict",
    )(data.reshape(parts, blocks, per, shots, traces), aperture, ops, cable_ops)
    if finish:
        return result.reshape(data.shape)
    result = jnp.swapaxes(result, 0, 1).reshape(data.shape)
    energy = lax.psum(jnp.sum(result * result, axis=(0, 1, 3)), "freq")
    scale = lax.rsqrt(energy / (2.0 * freqs * bands * traces) + 1e-06)
    return (result * scale[None, None, :, None]).astype(jnp.bfloat16)


def solution(mesh):
    return jax.shard_map(
        functools.partial(per_device, mesh.shape["shot"], mesh.shape["freq"]),
        mesh=mesh,
        in_specs=(P(None, "freq", "shot", None), P("shot", None), P(), P()),
        out_specs=P(None, "freq", "shot", None),
        check_vma=False,
    )
```

```python
import functools

import jax
import jax.numpy as jnp
from jax import lax
from jax.experimental import pallas as pl
from jax.experimental.pallas import tpu as pltpu
from jax.sharding import PartitionSpec as P

MESH = pl.DeviceIdType.MESH


def kernel(
    n, groups, chunks, finish, data, aperture, ops, cable_ops, out,
    dbuf, apbuf, opsbuf, idbuf, maskbuf, recv, maskrecv, send, back,
    local_sem, recv_sem, send_sem, mask_send_sem, mask_recv_sem, back_send_sem, back_recv_sem, team_sem,
):
    me = lax.axis_index("shot")
    parts, blocks, per, shots, traces = data.shape
    team = n // groups
    freqs = blocks * per
    total, rows = n * shots, team * shots
    cables = cable_ops.shape[0]
    width = ops.shape[1]
    seat = lax.rem(me, team)
    first = me - seat

    flips = []
    for place in (1 << k for k in range(n.bit_length() - 1)):
        flips.append((place, place * (1 - 2 * lax.rem(me // place, 2))))

    def partner(m):
        return me + sum(flip for place, flip in flips if m & place)

    def partner_seat(m):
        return seat + sum(flip for place, flip in flips if m & place and place < team)

    barrier = pltpu.get_barrier_semaphore()
    for m in reversed(range(team, n)):
        pl.semaphore_signal(barrier, inc=1, device_id={"shot": partner(m)}, device_id_type=MESH)

    fetches = [
        pltpu.make_async_copy(aperture, apbuf, local_sem.at[0]),
        pltpu.make_async_copy(ops, opsbuf, local_sem.at[1]),
    ] + [pltpu.make_async_copy(data.at[p], dbuf.at[:, p], local_sem.at[2 + p]) for p in range(parts)]
    fetches.append(pltpu.make_async_copy(cable_ops, idbuf, local_sem.at[2 + parts]))
    for fetch in fetches:
        fetch.start()

    fetches[0].wait()
    lists = apbuf[...]
    surface = lax.broadcasted_iota(jnp.int32, (shots, total), 1)
    found = jnp.zeros((shots, total), jnp.float32)
    for a in range(lists.shape[1]):
        found = jnp.where(lists[:, a : a + 1] == surface, 1.0, found)
    maskbuf[...] = found.astype(jnp.bfloat16)
    for fetch in fetches[1:]:
        fetch.wait()

    pl.semaphore_wait(barrier, n - team)
    pl.semaphore_signal(team_sem, inc=1, device_id={"shot": partner(team)}, device_id_type=MESH)

    def block(chunk, peer_seat):
        return dbuf.at[peer_seat * chunks + chunk]

    def scatter(chunk, peer_seat, peer):
        pltpu.make_async_remote_copy(
            src_ref=block(chunk, peer_seat), dst_ref=recv.at[chunk, me],
            send_sem=send_sem, recv_sem=recv_sem.at[chunk],
            device_id={"shot": peer}, device_id_type=MESH,
        ).start()

    for chunk in range(chunks):
        for m in reversed(range(1, n)):
            if chunk == 0 and m == team - 1:
                pl.semaphore_wait(team_sem, 1)
            if chunk == 0 and m < team:
                pltpu.make_async_remote_copy(
                    src_ref=maskbuf, dst_ref=maskrecv.at[seat],
                    send_sem=mask_send_sem, recv_sem=mask_recv_sem,
                    device_id={"shot": partner(m)}, device_id_type=MESH,
                ).start()
            scatter(chunk, partner_seat(m), partner(m))
        if chunk == 0:
            pltpu.make_async_copy(maskbuf, maskrecv.at[seat], mask_recv_sem).start()
        pltpu.make_async_copy(block(chunk, seat), recv.at[chunk, me], recv_sem.at[chunk]).start()

    lines = []
    for c in range(cables):
        pieces = [jnp.zeros((width, width), jnp.float32)] * cables
        pieces[c] = opsbuf[idbuf[c]].astype(jnp.float32)
        lines.append(jnp.concatenate(pieces, axis=1))
    operator = jnp.concatenate(lines, axis=0).astype(jnp.bfloat16)

    pltpu.make_async_copy(maskrecv, maskrecv, mask_recv_sem).wait()
    mask = maskrecv[...].astype(jnp.float32).reshape(rows, total)

    for chunk in range(chunks):
        pltpu.make_async_copy(recv.at[chunk], recv.at[chunk], recv_sem.at[chunk]).wait()
        for f in range(per):
            real = recv[chunk, :, 0, f].astype(jnp.float32).reshape(total, traces)
            imag = recv[chunk, :, 1, f].astype(jnp.float32).reshape(total, traces)
            if groups == 1:
                own_real, own_imag = real, imag
            else:
                own_real = recv[chunk, pl.ds(first, team), 0, f].astype(jnp.float32).reshape(rows, traces)
                own_imag = recv[chunk, pl.ds(first, team), 1, f].astype(jnp.float32).reshape(rows, traces)
            left = jnp.concatenate([own_real * mask, own_imag * mask], axis=1).astype(jnp.bfloat16)
            right = jnp.concatenate(
                [jnp.concatenate([real, imag], axis=1), jnp.concatenate([-imag, real], axis=1)], axis=0
            ).astype(jnp.bfloat16)
            product = jnp.dot(left, right, preferred_element_type=jnp.float32)
            product = jnp.concatenate([product[:, :traces], product[:, traces:]], axis=0)
            high = product.astype(jnp.bfloat16)
            rest = product - high.astype(jnp.float32)
            middle = rest.astype(jnp.bfloat16)
            low = (rest - middle.astype(jnp.float32)).astype(jnp.bfloat16)
            result = jnp.dot(low, operator, preferred_element_type=jnp.float32)
            result += jnp.dot(middle, operator, preferred_element_type=jnp.float32)
            result += jnp.dot(high, operator, preferred_element_type=jnp.float32)
            result = result.reshape(parts, team, shots, traces)
            for p in range(parts):
                send[chunk, :, p, f] = result[p]

        landing = back.at[seat * chunks + chunk]

        for m in reversed(range(1, team)):
            pltpu.make_async_remote_copy(
                src_ref=send.at[chunk, partner_seat(m)], dst_ref=landing,
                send_sem=back_send_sem, recv_sem=back_recv_sem,
                device_id={"shot": partner(m)}, device_id_type=MESH,
            ).start()
        pltpu.make_async_copy(send.at[chunk, seat], landing, back_recv_sem).start()

    mask_sent = maskrecv.at[pl.ds(0, team - 1)]
    sent = recv.at[:, pl.ds(0, n - 1)]
    back_sent = send.at[:, pl.ds(0, team - 1)]
    pltpu.make_async_copy(mask_sent, mask_sent, mask_send_sem).wait()
    pltpu.make_async_copy(sent, sent, send_sem).wait()
    pltpu.make_async_copy(back, back, back_recv_sem).wait()
    if finish:
        predicted = back[...]
        energy = jnp.sum(jnp.sum(predicted * predicted, axis=(0, 1, 2)), axis=1, keepdims=True)
        scale = lax.rsqrt(energy / (2.0 * freqs * traces) + 1e-06)
        for p in range(parts):
            out[p] = (back[:, p] * scale[None, None]).astype(out.dtype)
    pltpu.make_async_copy(back_sent, back_sent, back_send_sem).wait()


GROUPS = 2
CHUNKS = 2


def per_device(n, bands, data, aperture, ops, cable_ops):
    parts, freqs, shots, traces = data.shape
    groups, chunks = GROUPS, CHUNKS
    team = n // groups
    per = freqs // (team * chunks)
    finish = bands == 1
    dma = pltpu.SemaphoreType.DMA
    blocks = team * chunks
    held = (blocks, parts, per, shots, traces)
    shape = (parts, blocks, per, shots, traces) if finish else held
    scratch = [
        pltpu.VMEM(held, data.dtype),
        pltpu.VMEM(aperture.shape, aperture.dtype),
        pltpu.VMEM(ops.shape, ops.dtype),
        pltpu.SMEM(cable_ops.shape, cable_ops.dtype),
        pltpu.VMEM((shots, n * shots), jnp.bfloat16),
        pltpu.VMEM((chunks, n, parts, per, shots, traces), jnp.bfloat16),
        pltpu.VMEM((team, shots, n * shots), jnp.bfloat16),
        pltpu.VMEM((chunks, team, parts, per, shots, traces), jnp.float32),
    ]
    sems = [dma((3 + parts,)), dma((chunks,))] + [dma] * 5 + [pltpu.SemaphoreType.REGULAR]
    anywhere = pl.BlockSpec(memory_space=pl.ANY)
    body = functools.partial(kernel, n, groups, chunks, finish)
    if finish:
        scratch.append(pltpu.VMEM(held, jnp.float32))
        out_dtype = jnp.bfloat16
    else:
        inner = body

        def body(data, aperture, ops, cable_ops, out, *rest):
            place = len(scratch)
            inner(data, aperture, ops, cable_ops, out, *rest[:place], out, *rest[place:])

        out_dtype = jnp.float32
    result = pl.pallas_call(
        body,
        out_shape=pltpu.VMEM(shape, out_dtype),
        in_specs=[anywhere] * 4,
        out_specs=pl.BlockSpec(memory_space=pltpu.VMEM),
        scratch_shapes=scratch + sems,
        compiler_params=pltpu.CompilerParams(collective_id=0, has_side_effects=True),
        name="predict",
    )(data.reshape(parts, blocks, per, shots, traces), aperture, ops, cable_ops)
    if finish:
        return result.reshape(data.shape)
    result = jnp.swapaxes(result, 0, 1).reshape(data.shape)
    energy = lax.psum(jnp.sum(result * result, axis=(0, 1, 3)), "freq")
    scale = lax.rsqrt(energy / (2.0 * freqs * bands * traces) + 1e-06)
    return (result * scale[None, None, :, None]).astype(jnp.bfloat16)


def solution(mesh):
    return jax.shard_map(
        functools.partial(per_device, mesh.shape["shot"], mesh.shape["freq"]),
        mesh=mesh,
        in_specs=(P(None, "freq", "shot", None), P("shot", None), P(), P()),
        out_specs=P(None, "freq", "shot", None),
        check_vma=False,
    )
```
